32 devices in a mesh: view: 4 (over y, x), blk: 8 (over z, core).
Axes of the slice: x: 2, y: 2, z: 4, core: 2. Of those that a mesh axis runs over, the one named last changes fastest.
Arguments:
- estimate: float32 [384, 64, 256], P('blk'), may hold values from 0.5 to 2
- views_seen: float32 [4, 384, 64, 256], P('view', 'blk'), may hold values from 0.2 to 5
- weight_mask: int32 [4, 384, 64, 256], P('view', 'blk'), may hold values from 1 to 3
- psf: float32 [4, 3, 21], P('view'), may hold values from 0.05 to 1
Outputs:
- joined: float32 [384, 64, 256], P('blk')
The draws below stay inside these ranges and needn't reach their ends.
All inputs are finite; a program needn't handle non-finite values.
Results may differ from the reference program's by a relative error of at most 0.0001.
Values sent between devices are 32-bit elements; how exact they have to be, the bound alone decides.
A program may use at most 128 MiB of HBM per device.

```python
import math
import jax
import jax.numpy as jnp
from jax import lax

CY = 64
CZ = 256
TAPS = 21
ITERS = 2
VIEWS = 4
NX = 384


def plant(values, own_key, smallest, high):
    place = [jax.random.randint(jax.random.fold_in(own_key, axis), (), 0, length) for axis, length in enumerate(values.shape)]
    widest = values.shape.index(max(values.shape))
    next_to = place[:widest] + [(place[widest] + 1) % values.shape[widest]] + place[widest + 1:]
    return values.at[tuple(place)].set(smallest).at[tuple(next_to)].set(high)


def levels(rng, dims, cuts, least, top_value):
    gain = 1.0
    for dim, parts in cuts:
        heights = jax.random.uniform(jax.random.fold_in(jax.random.fold_in(rng, 6), dim), (parts,), jnp.float32, least / len(cuts), top_value / len(cuts))
        gain = gain * jnp.repeat(jnp.exp(heights), dims[dim] // parts).reshape((-1,) + (1,) * (len(dims) - 1 - dim))
    return gain


def setup_inputs(seed: int = 0) -> dict:
    seeds = jax.random.split(jax.random.key(seed), 5)
    return {
        "estimate": jnp.clip(0.5 + 1.5 * jax.random.uniform(seeds[0], (NX, CY, CZ), jnp.float32) ** levels(seeds[0], (NX, CY, CZ), ((0, 8),), -0.2, 0.2), 0.5, 2.0),
        "views_seen": jnp.clip(jnp.exp(math.log(5.0) - 3.218876 * jax.random.uniform(seeds[1], (VIEWS, NX, CY, CZ), jnp.float32) ** levels(seeds[1], (VIEWS, NX, CY, CZ), ((0, 4), (1, 8)), -0.2, 0.2)), 0.2, 5.0),
        "weight_mask": plant(jax.random.randint(seeds[2], (VIEWS, NX, CY, CZ), 1, 4), jax.random.fold_in(seeds[2], 1), 1, 3).astype(jnp.int32),
        "psf": jnp.clip(jnp.exp(math.log(1.0) - 2.9957323 * jax.random.uniform(seeds[3], (VIEWS, 3, TAPS), jnp.float32) ** levels(seeds[3], (VIEWS, 3, TAPS), ((0, 4),), -0.2, 0.2)), 0.05, 1.0),
    }


def band_matrix(kernel, out_count, in_count, offset_by):
    row_index = jnp.arange(out_count)[:, None]
    col_index = jnp.arange(in_count)[None, :]
    offset_table = col_index - row_index + offset_by
    matches = offset_table[:, :, None] == jnp.arange(kernel.shape[0])[None, None, :]
    return jnp.sum(jnp.where(matches, kernel[None, None, :], 0.0), axis=-1)


def sweep_first(padded, kernel, count):
    result = kernel[0] * padded[0:count]
    for tap in range(1, kernel.shape[0]):
        result = result + kernel[tap] * padded[tap:tap + count]
    return result


def sweep_rest(volume, kernel):
    radius = (kernel.shape[-1] - 1) // 2
    along_y = band_matrix(kernel[1], volume.shape[1], volume.shape[1], radius)
    volume = jnp.einsum('ij,xjz->xiz', along_y, volume, precision=lax.Precision.HIGHEST)
    along_z = band_matrix(kernel[2], volume.shape[2], volume.shape[2], radius)
    return jnp.einsum('xyj,kj->xyk', volume, along_z, precision=lax.Precision.HIGHEST)


def blur_volume(volume, kernel):
    radius = (kernel.shape[-1] - 1) // 2
    padded = jnp.pad(volume, ((radius, radius), (0, 0), (0, 0)))
    return sweep_rest(sweep_first(padded, kernel[0], volume.shape[0]), kernel)


def reference(estimate, views_seen, weight_mask, psf):
    normed = psf / jnp.sum(psf, axis=-1, keepdims=True)
    flipped = normed[:, :, ::-1]
    weights_all = jnp.sum(weight_mask.astype(jnp.float32), axis=0)
    for iteration in range(ITERS):
        current = estimate

        def add_view(running, pieces):
            observed, view_mask, forward, backward = pieces
            blurred = blur_volume(current, forward)
            correction = blur_volume(observed / blurred, backward)
            return running + view_mask.astype(jnp.float32) * correction, None

        numerator, _ = lax.scan(add_view, jnp.zeros_like(estimate), (views_seen, weight_mask, normed, flipped))
        estimate = estimate * numerator / weights_all
    return estimate
```

```python
import functools

import jax
import jax.numpy as jnp
from jax import lax
from jax.experimental import pallas as pl
from jax.experimental.pallas import tpu as pltpu
from jax.sharding import PartitionSpec as P

ITERS = 2
CHUNKS = 8
MESH = pl.DeviceIdType.MESH
F32, BF16 = jnp.float32, jnp.bfloat16


def split(value):
    high = value.astype(BF16)
    return high, (value - high.astype(F32)).astype(BF16)


def band(taps, row, size, row_sign, scale):
    rows = lax.broadcasted_iota(jnp.int32, (size, size), 0)
    cols = lax.broadcasted_iota(jnp.int32, (size, size), 1)
    count = taps.shape[2]
    offset = (cols - rows) * row_sign + (count - 1) // 2
    total = jnp.zeros((size, size), F32)
    for k in range(count):
        total = jnp.where(offset == k, taps[0, row, k], total)
    return split(total * scale)


def kernel(dims, taps, est_in, seen_in, mask_in, out,
           ext, seen, mask, wsum, nums, recvs, xbuf, ymats, zmats,
           mask_sem, load_sem, halo_send, halo_recv, rs_send, rs_recv, ag_send, ag_recv):
    views, blks, bits = dims
    slab, cy, cz = seen.shape
    count = taps.shape[2]
    rad = (count - 1) // 2
    chunks = CHUNKS
    chunk = slab // chunks
    half = chunks // 2
    order = [t // 2 if t % 2 == 0 else chunks - 1 - t // 2 for t in range(chunks)]
    turn = [order.index(c) % bits for c in range(chunks)]
    v, b = lax.axis_index("view"), lax.axis_index("blk")
    bit = [(v // 2**p) % 2 for p in range(bits)]
    partner = [v + (1 - 2 * bit[p]) * 2**p for p in range(bits)]
    left, right = (b + blks - 1) % blks, (b + 1) % blks

    def planes(p):
        return pl.ds(p * chunk, chunk)

    mask_loads = [
        pltpu.make_async_copy(mask_in.at[0, planes(p)], mask.at[planes(p)], mask_sem.at[p])
        for p in range(chunks)
    ]
    loads = [
        pltpu.make_async_copy(est_in, ext.at[0, pl.ds(rad, slab)], load_sem.at[0]),
        pltpu.make_async_copy(seen_in.at[0], seen, load_sem.at[1]),
    ]
    for p in order:
        mask_loads[p].start()
    for load in loads:
        load.start()

    barrier = pltpu.get_barrier_semaphore()
    for p in range(bits):
        pl.semaphore_signal(barrier, inc=1, device_id=(partner[p], b), device_id_type=MESH)
    for near in (left, right):
        pl.semaphore_signal(barrier, inc=1, device_id=(v, near), device_id_type=MESH)
    pl.semaphore_wait(barrier, bits + 2)

    def halo(which, side):
        start, land, near = ((slab, 0, right), (rad, rad + slab, left))[side]
        src = ext.at[which, pl.ds(start, rad)] if which else est_in.at[pl.ds(start - rad, rad)]
        return pltpu.make_async_remote_copy(
            src_ref=src, dst_ref=ext.at[which, pl.ds(land, rad)],
            send_sem=halo_send.at[which, side], recv_sem=halo_recv.at[which, side],
            device_id=(v, near), device_id_type=MESH)

    def halo_start(which):
        @pl.when(b < blks - 1)
        def _():
            halo(which, 0).start()

        @pl.when(b > 0)
        def _():
            halo(which, 1).start()

    def halo_wait(which):
        @pl.when(b > 0)
        def _():
            halo(which, 0).wait_recv()

        @pl.when(b == 0)
        def _():
            ext[which, pl.ds(0, rad)] = jnp.zeros((rad, cy, cz), F32)

        @pl.when(b < blks - 1)
        def _():
            halo(which, 1).wait_recv()

        @pl.when(b == blks - 1)
        def _():
            ext[which, pl.ds(rad + slab, rad)] = jnp.zeros((rad, cy, cz), F32)

    def halo_sent(which):
        @pl.when(b < blks - 1)
        def _():
            halo(which, 0).wait_send()

        @pl.when(b > 0)
        def _():
            halo(which, 1).wait_send()

    def way(p, s):
        return (turn[p] + s) % bits

    def region(p, s):
        start, length = 0, cy
        for t in range(s):
            length //= 2
            start = start + bit[way(p, t)] * length
        return start, length

    def lines(start, length):
        if not isinstance(start, int):
            start = pl.multiple_of(start, 8)
        return pl.ds(start, length)

    def rs_copy(r, s, p):
        buf = wsum if r == 0 else nums.at[r - 1]
        start, length = region(p, s)
        length //= 2
        mine = bit[way(p, s)]
        return pltpu.make_async_remote_copy(
            src_ref=buf.at[planes(p), lines(start + (1 - mine) * length, length)],
            dst_ref=recvs.at[r, planes(p), pl.ds(cy - cy // 2**s, length)],
            send_sem=rs_send.at[r, s, p], recv_sem=rs_recv.at[r, s, p],
            device_id=(partner[way(p, s)], b), device_id_type=MESH)

    def rs_take(r, s, p):
        buf = wsum if r == 0 else nums.at[r - 1]
        rs_copy(r, s, p).wait_recv()
        start, length = region(p, s + 1)
        kept, came = lines(start, length), pl.ds(cy - cy // 2**s, length)

        def add(i, carry):
            cell = p * chunk + i
            buf[cell, kept] = buf[cell, kept] + recvs[r, cell, came]
            return carry

        lax.fori_loop(0, chunk, add, 0)

    def ag_copy(r, s, p):
        start, length = region(p, s + 1)
        if r < ITERS - 1:
            ref = ext.at[2 * (r + 1), pl.ds(p * chunk + rad, chunk), lines(start, length)]
        else:
            ref = out.at[planes(p), lines(start, length)]
        return pltpu.make_async_remote_copy(
            src_ref=ref, dst_ref=ref,
            send_sem=ag_send.at[r, s, p], recv_sem=ag_recv.at[r, s, p],
            device_id=(partner[way(p, s)], b), device_id_type=MESH)

    def blur(which, c, back):
        first = c * chunk

        height, lanes = 8, 256

        def block(j, carry):
            line = pl.multiple_of((j // (cz // lanes)) * height, height)
            column = pl.multiple_of((j % (cz // lanes)) * lanes, lanes)
            window = (pl.ds(line, height), pl.ds(column, lanes))
            totals = [None] * chunk
            for k in range(count + chunk - 1):
                plane = ext[(which, first + k) + window]
                for i in range(max(0, k - count + 1), min(chunk, k + 1)):
                    tap = k - i
                    term = taps[0, 0, count - 1 - tap if back else tap] * plane
                    totals[i] = term if totals[i] is None else totals[i] + term
            for i in range(chunk):
                xbuf[(i,) + window] = totals[i]
            return carry

        lax.fori_loop(0, (cy // height) * (cz // lanes), block, 0)
        blurred = []
        for i in range(chunk):
            high, low = split(xbuf[i])
            stack = jnp.concatenate([high, high, low], axis=0)
            blurred.append(jnp.dot(ymats[back], stack, preferred_element_type=F32))
        high, low = split(jnp.concatenate(blurred, axis=0))
        high_mat, low_mat = zmats[back, 0], zmats[back, 1]
        result = jnp.dot(high, high_mat, preferred_element_type=F32)
        result += jnp.dot(low, high_mat, preferred_element_type=F32)
        result += jnp.dot(high, low_mat, preferred_element_type=F32)
        return result.reshape(chunk, cy, cz)

    def over(step, first, last, inward=True):
        def run(t, carry):
            t = t if inward else chunks - 1 - t
            step((t % 2) * (chunks - 1) + (1 - 2 * (t % 2)) * (t // 2))
            return carry

        lax.fori_loop(first, last, run, 0)

    halo_start(0)
    for p in order:
        mask_loads[p].wait()

        def to_float(i, carry):
            wsum[p * chunk + i] = mask[p * chunk + i].astype(F32)
            return carry

        lax.fori_loop(0, chunk, to_float, 0)
        rs_copy(0, 0, p).start()

    sums = []
    for row in range(3):
        total = taps[0, row, 0]
        for k in range(1, count):
            total = total + taps[0, row, k]
        sums.append(jnp.full((1, cz), total, F32))
    y_scale = (1.0 / (sums[0] * sums[1]))[:, :cy]
    z_scale = 1.0 / sums[2]
    for back in range(2):
        sign = -1 if back else 1
        high, low = band(taps, 1, cy, sign, y_scale)
        ymats[back] = jnp.concatenate([high, low, high], axis=1)
        high, low = band(taps, 2, cz, -sign, z_scale)
        zmats[back, 0] = high
        zmats[back, 1] = low
    for load in loads:
        load.wait()

    def quotient(r):
        def step(c):
            blurred = blur(2 * r, c, 0)
            ext[2 * r + 1, pl.ds(rad + c * chunk, chunk)] = seen[planes(c)] / blurred

        return step

    def correct(r, send):
        def step(c):
            corrected = blur(2 * r + 1, c, 1)
            rows = planes(c)
            nums[r, rows] = mask[rows].astype(F32) * corrected
            if send:
                for p in range(chunks):
                    @pl.when(c == p)
                    def _(p=p):
                        rs_copy(r + 1, 0, p).start()

        return step

    def update(r, p):
        start, length = region(p, bits)
        kept = lines(start, length)

        def cells(i, carry):
            cell = p * chunk + i
            fresh = ext[2 * r, rad + cell, kept] * nums[r, cell, kept] / wsum[cell, kept]
            if r < ITERS - 1:
                ext[2 * r + 2, rad + cell, kept] = fresh
            else:
                out[cell, kept] = fresh
            return carry

        lax.fori_loop(0, chunk, cells, 0)

    def event(r, e, p):
        if e < bits:
            rs_take(r + 1, e, p)
            if e + 1 < bits:
                rs_copy(r + 1, e + 1, p).start()
            else:
                update(r, p)
                ag_copy(r, bits - 1, p).start()
        else:
            s = 2 * bits - 1 - e
            ag_copy(r, s, p).wait_recv()
            if s > 0:
                ag_copy(r, s - 1, p).start()

    def events(r, e, group):
        for p in group:
            event(r, e, p)

    need = -(-rad // chunk)
    for r in range(ITERS):
        here, there = 2 * r, 2 * r + 1
        last_r = r == ITERS - 1
        if r == 0:
            over(quotient(r), half, chunks)
            halo_wait(here)
            over(quotient(r), 0, half)
            halo_start(there)
        else:
            over(quotient(r), 2, half)
            halo_start(there)
            over(quotient(r), half, chunks)

        over(correct(r, last_r), 0, half, inward=False)
        if r == 0:
            for p in order:
                rs_take(0, 0, p)
                if bits > 1:
                    rs_copy(0, 1, p).start()
        halo_wait(there)
        if last_r:
            over(correct(r, True), half, chunks, inward=False)
        else:
            over(correct(r, r > 0), 0, half)
        if r == 0:
            for p in order[:half]:
                rs_copy(1, 0, p).start()
            for s in range(1, bits):
                for p in order:
                    rs_take(0, s, p)
                    if s + 1 < bits:
                        rs_copy(0, s + 1, p).start()

        if last_r:
            sequence = order[::-1]
            for e in range(2 * bits):
                events(r, e, sequence)
        else:
            first, second = order[:half], order[half:]
            quarter = half // 2
            events(r, 0, first)
            for p in second[:quarter]:
                rs_copy(r + 1, 0, p).start()
            events(r, 1, first)
            for p in second[quarter:]:
                rs_copy(r + 1, 0, p).start()
            for e in range(2, 2 * bits):
                if e == 2 * bits - 1:
                    events(r, 0, second[:quarter])
                events(r, e, first)
            halo_start(here + 2)
            events(r, 0, second[quarter:])
            for e in range(1, 2 * bits - 1):
                events(r, e, second)
            events(r, 2 * bits - 1, second[:quarter])
            halo_wait(here + 2)
            over(quotient(r + 1), 0, 2)
            events(r, 2 * bits - 1, second[quarter:])

    for which in range(2 * ITERS):
        halo_sent(which)
    for s in range(bits):
        for p in range(chunks):
            for r in range(ITERS + 1):
                rs_copy(r, s, p).wait_send()
            for r in range(ITERS):
                ag_copy(r, s, p).wait_send()


def body(views, blks, estimate, views_seen, weight_mask, psf):
    slab, cy, cz = estimate.shape
    bits = views.bit_length() - 1
    hbm = pl.BlockSpec(memory_space=pl.ANY)
    vmem = pltpu.VMEM
    dma = pltpu.SemaphoreType.DMA
    count = psf.shape[-1]
    rad = (count - 1) // 2
    chunks = CHUNKS
    return pl.pallas_call(
        functools.partial(kernel, (views, blks, bits)),
        out_shape=vmem(estimate.shape, F32),
        in_specs=[pl.BlockSpec(memory_space=pltpu.SMEM), hbm, hbm, hbm],
        out_specs=pl.BlockSpec(memory_space=vmem),
        scratch_shapes=[
            vmem((2 * ITERS, slab + 2 * rad, cy, cz), F32),
            vmem((slab, cy, cz), F32),
            vmem((slab, cy, cz), jnp.int32),
            vmem((slab, cy, cz), F32),
            vmem((ITERS, slab, cy, cz), F32),
            vmem((ITERS + 1, slab, cy - cy // views, cz), F32),
            vmem((slab // chunks, cy, cz), F32),
            vmem((2, cy, 3 * cy), BF16),
            vmem((2, 2, cz, cz), BF16),
            dma((chunks,)),
            dma((2,)),
            dma((2 * ITERS, 2)),
            dma((2 * ITERS, 2)),
            dma((ITERS + 1, bits, chunks)),
            dma((ITERS + 1, bits, chunks)),
            dma((ITERS, bits, chunks)),
            dma((ITERS, bits, chunks)),
        ],
        compiler_params=pltpu.CompilerParams(
            collective_id=0, has_side_effects=True, vmem_limit_bytes=56 * 2**20),
    )(psf, estimate, views_seen, weight_mask)


def solution(mesh):
    placed = (
        P("blk", None, None),
        P("view", "blk", None, None),
        P("view", "blk", None, None),
        P("view", None, None),
    )
    return jax.shard_map(
        functools.partial(body, mesh.shape["view"], mesh.shape["blk"]),
        mesh=mesh, in_specs=placed, out_specs=P("blk", None, None), check_vma=False
    )
```

```python
import functools

import jax
import jax.numpy as jnp
from jax import lax
from jax.experimental import pallas as pl
from jax.experimental.pallas import tpu as pltpu
from jax.sharding import PartitionSpec as P

ITERS = 2
CHUNKS = 8
MESH = pl.DeviceIdType.MESH
F32, BF16 = jnp.float32, jnp.bfloat16


def split(value):
    high = value.astype(BF16)
    return high, (value - high.astype(F32)).astype(BF16)


def band(taps, row, size, row_sign, scale):
    rows = lax.broadcasted_iota(jnp.int32, (size, size), 0)
    cols = lax.broadcasted_iota(jnp.int32, (size, size), 1)
    count = taps.shape[2]
    offset = (cols - rows) * row_sign + (count - 1) // 2
    total = jnp.zeros((size, size), F32)
    for k in range(count):
        total = jnp.where(offset == k, taps[row, 0, k], total)
    return split(total * scale)


def kernel(dims, taps, est_in, seen_in, mask_in, out,
           est, ext, seen, mask, wsum, nums, recvs, xbuf, ymats, zmats,
           mask_sem, load_sem, halo_send, halo_recv, rs_send, rs_recv, ag_send, ag_recv):
    views, blks, bits = dims
    slab, cy, cz = seen.shape
    count = taps.shape[2]
    rad = (count - 1) // 2
    chunks = CHUNKS
    chunk = slab // chunks
    half = chunks // 2
    order = [t // 2 if t % 2 == 0 else chunks - 1 - t // 2 for t in range(chunks)]
    turn = [order.index(c) % bits for c in range(chunks)]
    v, b = lax.axis_index("view"), lax.axis_index("blk")
    bit = [(v // 2**p) % 2 for p in range(bits)]
    partner = [v + (1 - 2 * bit[p]) * 2**p for p in range(bits)]
    left, right = (b + blks - 1) % blks, (b + 1) % blks

    def planes(p):
        return pl.ds(p * chunk, chunk)

    mask_loads = [
        pltpu.make_async_copy(mask_in.at[0, planes(p)], mask.at[planes(p)], mask_sem.at[p])
        for p in range(chunks)
    ]
    loads = [
        pltpu.make_async_copy(est_in, ext.at[0, pl.ds(rad, slab)], load_sem.at[0]),
        pltpu.make_async_copy(seen_in.at[0], seen, load_sem.at[1]),
    ]
    for p in order:
        mask_loads[p].start()
    for load in loads:
        load.start()

    barrier = pltpu.get_barrier_semaphore()
    for p in range(bits):
        pl.semaphore_signal(barrier, inc=1, device_id=(partner[p], b), device_id_type=MESH)
    for near in (left, right):
        pl.semaphore_signal(barrier, inc=1, device_id=(v, near), device_id_type=MESH)
    pl.semaphore_wait(barrier, bits + 2)

    def halo(which, side):
        start, land, near = ((slab, 0, right), (rad, rad + slab, left))[side]
        src = ext.at[which, pl.ds(start, rad)] if which else est_in.at[pl.ds(start - rad, rad)]
        return pltpu.make_async_remote_copy(
            src_ref=src, dst_ref=ext.at[which, pl.ds(land, rad)],
            send_sem=halo_send.at[which, side], recv_sem=halo_recv.at[which, side],
            device_id=(v, near), device_id_type=MESH)

    def halo_start(which):
        @pl.when(b < blks - 1)
        def _():
            halo(which, 0).start()

        @pl.when(b > 0)
        def _():
            halo(which, 1).start()

    def halo_wait(which):
        @pl.when(b > 0)
        def _():
            halo(which, 0).wait_recv()

        @pl.when(b == 0)
        def _():
            ext[which, pl.ds(0, rad)] = jnp.zeros((rad, cy, cz), F32)

        @pl.when(b < blks - 1)
        def _():
            halo(which, 1).wait_recv()

        @pl.when(b == blks - 1)
        def _():
            ext[which, pl.ds(rad + slab, rad)] = jnp.zeros((rad, cy, cz), F32)

    def halo_sent(which):
        @pl.when(b < blks - 1)
        def _():
            halo(which, 0).wait_send()

        @pl.when(b > 0)
        def _():
            halo(which, 1).wait_send()

    def way(p, s):
        return (turn[p] + s) % bits

    def region(p, s):
        start, length = 0, cy
        for t in range(s):
            length //= 2
            start = start + bit[way(p, t)] * length
        return start, length

    def lines(start, length):
        if not isinstance(start, int):
            start = pl.multiple_of(start, 8)
        return pl.ds(start, length)

    def rs_copy(r, s, p):
        buf = wsum if r == 0 else nums.at[r - 1]
        start, length = region(p, s)
        length //= 2
        mine = bit[way(p, s)]
        return pltpu.make_async_remote_copy(
            src_ref=buf.at[planes(p), lines(start + (1 - mine) * length, length)],
            dst_ref=recvs.at[r, planes(p), pl.ds(cy - cy // 2**s, length)],
            send_sem=rs_send.at[r, s, p], recv_sem=rs_recv.at[r, s, p],
            device_id=(partner[way(p, s)], b), device_id_type=MESH)

    def rs_take(r, s, p):
        buf = wsum if r == 0 else nums.at[r - 1]
        rs_copy(r, s, p).wait_recv()
        start, length = region(p, s + 1)
        kept, came = lines(start, length), pl.ds(cy - cy // 2**s, length)

        def add(i, carry):
            cell = p * chunk + i
            buf[cell, kept] = buf[cell, kept] + recvs[r, cell, came]
            return carry

        lax.fori_loop(0, chunk, add, 0)

    def ag_copy(r, s, p):
        start, length = region(p, s + 1)
        if r < ITERS - 1:
            ref = est.at[r, planes(p), lines(start, length)]
        else:
            ref = out.at[planes(p), lines(start, length)]
        return pltpu.make_async_remote_copy(
            src_ref=ref, dst_ref=ref,
            send_sem=ag_send.at[r, s, p], recv_sem=ag_recv.at[r, s, p],
            device_id=(partner[way(p, s)], b), device_id_type=MESH)

    def windows(step):
        height = 8

        def run(j, carry):
            step((pl.ds(pl.multiple_of(j * height, height), height), slice(None)))
            return carry

        lax.fori_loop(0, cy // height, run, 0)

    def sweep(which, first, window, back, keep=None):
        totals = [None] * chunk
        for k in range(count + chunk - 1):
            if keep is not None and not keep(k):
                continue
            plane = ext[(which, first + k) + window]
            for i in range(max(0, k - count + 1), min(chunk, k + 1)):
                tap = k - i
                term = taps[0, 0, count - 1 - tap if back else tap] * plane
                totals[i] = term if totals[i] is None else totals[i] + term
        return totals

    def in_plane(cells, back):
        blurred = []
        for cell in cells:
            high, low = split(cell)
            stack = jnp.concatenate([high, high, low], axis=0)
            blurred.append(jnp.dot(ymats[back], stack, preferred_element_type=F32))
        high, low = split(jnp.concatenate(blurred, axis=0))
        high_mat, low_mat = zmats[back, 0], zmats[back, 1]
        result = jnp.dot(high, high_mat, preferred_element_type=F32)
        result += jnp.dot(low, high_mat, preferred_element_type=F32)
        result += jnp.dot(high, low_mat, preferred_element_type=F32)
        result = result.reshape(2, chunk, cy, cz)
        return result[0], result[1]

    def pair(t):
        return t, chunks - 1 - t

    def blur(which, t, back):
        for side, c in enumerate(pair(t)):
            def rows(window, side=side, c=c):
                totals = sweep(which, c * chunk, window, back)
                for i in range(chunk):
                    xbuf[(side * chunk + i,) + window] = totals[i]

            windows(rows)
        return in_plane([xbuf[i] for i in range(2 * chunk)], back)

    def over(step, first, last, inward=True):
        def run(t, carry):
            step(t if inward else half - 1 - t)
            return carry

        lax.fori_loop(first, last, run, 0)

    halo_start(0)
    for p in order:
        mask_loads[p].wait()

        def to_float(i, carry):
            wsum[p * chunk + i] = mask[p * chunk + i].astype(F32)
            return carry

        lax.fori_loop(0, chunk, to_float, 0)
        rs_copy(0, 0, p).start()

    sums = []
    for row in range(3):
        total = taps[row, 0, 0]
        for k in range(1, count):
            total = total + taps[row, 0, k]
        sums.append(jnp.full((1, cz), total, F32))
    y_scale = (1.0 / (sums[0] * sums[1]))[:, :cy]
    z_scale = 1.0 / sums[2]
    for back in range(2):
        sign = -1 if back else 1
        high, low = band(taps, 1, cy, sign, y_scale)
        ymats[back] = jnp.concatenate([high, low, high], axis=1)
        high, low = band(taps, 2, cz, -sign, z_scale)
        zmats[back, 0] = high
        zmats[back, 1] = low
    for load in loads:
        load.wait()

    def quotient(t):
        for c, blurred in zip(pair(t), blur(0, t, 0)):
            ext[1, pl.ds(rad + c * chunk, chunk)] = seen[planes(c)] / blurred

    def spread(r):
        def step(t):
            cells = [est[r - 1, c * chunk + i] for c in pair(t) for i in range(chunk)]
            for c, blurred in zip(pair(t), in_plane(cells, 0)):
                ext[2 * r, pl.ds(rad + c * chunk, chunk)] = blurred

        return step

    low_last, high_last = (half - 1) * chunk, (half + 1) * chunk

    def divide(r, c, part):
        def late(k):
            return low_last <= c * chunk + k - rad < high_last

        keep = {"all": None, "early": lambda k: not late(k), "late": late}[part]

        def rows(window):
            totals = sweep(2 * r, c * chunk, window, 0, keep)
            for i in range(chunk):
                cell = c * chunk + i
                place = (2 * r + 1, rad + cell) + window
                total = totals[i]
                if part == "late":
                    total = ext[place] if total is None else ext[place] + total
                elif total is None:
                    total = jnp.zeros((8, cz), F32)
                ext[place] = total if part == "early" else seen[(cell,) + window] / total

        windows(rows)

    def correct(r, send):
        def step(t):
            for c, corrected in zip(pair(t), blur(2 * r + 1, t, 1)):
                nums[r, planes(c)] = mask[planes(c)].astype(F32) * corrected
            if send:
                for u in range(half):
                    @pl.when(t == u)
                    def _(u=u):
                        for p in pair(u):
                            rs_copy(r + 1, 0, p).start()

        return step

    def update(r, p):
        start, length = region(p, bits)
        kept = lines(start, length)

        def cells(i, carry):
            cell = p * chunk + i
            old = est[r - 1, cell, kept] if r else ext[0, rad + cell, kept]
            fresh = old * nums[r, cell, kept] / wsum[cell, kept]
            if r < ITERS - 1:
                est[r, cell, kept] = fresh
            else:
                out[cell, kept] = fresh
            return carry

        lax.fori_loop(0, chunk, cells, 0)

    def event(r, e, p):
        if e < bits:
            rs_take(r + 1, e, p)
            if e + 1 < bits:
                rs_copy(r + 1, e + 1, p).start()
            else:
                update(r, p)
                ag_copy(r, bits - 1, p).start()
        else:
            s = 2 * bits - 1 - e
            ag_copy(r, s, p).wait_recv()
            if s > 0:
                ag_copy(r, s - 1, p).start()

    def events(r, e, group):
        for p in group:
            event(r, e, p)

    quarter = half // 2
    first, second = order[:half], order[half:]
    for r in range(ITERS):
        here, there = 2 * r, 2 * r + 1
        if r == 0:
            over(quotient, quarter, half)
            halo_wait(here)
            over(quotient, 0, quarter)
            halo_start(there)
            over(correct(r, False), 0, quarter, inward=False)
            for p in order:
                rs_take(0, 0, p)
                if bits > 1:
                    rs_copy(0, 1, p).start()
            halo_wait(there)
            over(correct(r, True), 0, quarter)
            for s in range(1, bits):
                for p in order:
                    rs_take(0, s, p)
                    if s + 1 < bits:
                        rs_copy(0, s + 1, p).start()
        else:
            over(spread(r), half - 1, half)
            for t in range(1, half):
                for c in pair(t):
                    divide(r, c, "late")
                if t == quarter - 1:
                    halo_start(there)
            over(correct(r, True), 0, quarter, inward=False)
            halo_wait(there)
            over(correct(r, True), quarter, half, inward=False)

        if r == ITERS - 1:
            for e in range(2 * bits):
                events(r, e, order[::-1])
        else:
            events(r, 0, first)
            for p in second[:quarter]:
                rs_copy(r + 1, 0, p).start()
            events(r, 1, first)
            for p in second[quarter:]:
                rs_copy(r + 1, 0, p).start()
            for e in range(2, 2 * bits):
                if e == 2 * bits - 1:
                    events(r, 0, second[:quarter])
                events(r, e, first)
            events(r, 0, second[quarter:])
            over(spread(r + 1), 0, quarter)
            halo_start(here + 2)
            for e in range(1, 2 * bits - 1):
                events(r, e, second)
            events(r, 2 * bits - 1, second[:quarter])
            over(spread(r + 1), quarter, half - 1)
            halo_wait(here + 2)
            for c in pair(0):
                divide(r + 1, c, "all")
            for t in range(1, half):
                for c in pair(t):
                    divide(r + 1, c, "early")
            events(r, 2 * bits - 1, second[quarter:])

    for which in range(2 * ITERS):
        halo_sent(which)
    for s in range(bits):
        for p in range(chunks):
            for r in range(ITERS + 1):
                rs_copy(r, s, p).wait_send()
            for r in range(ITERS):
                ag_copy(r, s, p).wait_send()


def body(views, blks, estimate, views_seen, weight_mask, psf):
    slab, cy, cz = estimate.shape
    bits = views.bit_length() - 1
    hbm = pl.BlockSpec(memory_space=pl.ANY)
    vmem = pltpu.VMEM
    dma = pltpu.SemaphoreType.DMA
    count = psf.shape[-1]
    rad = (count - 1) // 2
    chunks = CHUNKS
    return pl.pallas_call(
        functools.partial(kernel, (views, blks, bits)),
        out_shape=vmem(estimate.shape, F32),
        in_specs=[pl.BlockSpec(memory_space=pltpu.SMEM), hbm, hbm, hbm],
        out_specs=pl.BlockSpec(memory_space=vmem),
        scratch_shapes=[
            vmem((ITERS - 1, slab, cy, cz), F32),
            vmem((2 * ITERS, slab + 2 * rad, cy, cz), F32),
            vmem((slab, cy, cz), F32),
            vmem((slab, cy, cz), jnp.int32),
            vmem((slab, cy, cz), F32),
            vmem((ITERS, slab, cy, cz), F32),
            vmem((ITERS + 1, slab, cy - cy // views, cz), F32),
            vmem((2 * (slab // chunks), cy, cz), F32),
            vmem((2, cy, 3 * cy), BF16),
            vmem((2, 2, cz, cz), BF16),
            dma((chunks,)),
            dma((2,)),
            dma((2 * ITERS, 2)),
            dma((2 * ITERS, 2)),
            dma((ITERS + 1, bits, chunks)),
            dma((ITERS + 1, bits, chunks)),
            dma((ITERS, bits, chunks)),
            dma((ITERS, bits, chunks)),
        ],
        compiler_params=pltpu.CompilerParams(
            collective_id=0, has_side_effects=True, vmem_limit_bytes=56 * 2**20),
    )(jnp.transpose(psf, (1, 0, 2)), estimate, views_seen, weight_mask)


def solution(mesh):
    placed = (
        P("blk", None, None),
        P("view", "blk", None, None),
        P("view", "blk", None, None),
        P("view", None, None),
    )
    return jax.shard_map(
        functools.partial(body, mesh.shape["view"], mesh.shape["blk"]),
        mesh=mesh, in_specs=placed, out_specs=P("blk", None, None), check_vma=False
    )
```

```python
import functools

import jax
import jax.numpy as jnp
from jax import lax
from jax.experimental import pallas as pl
from jax.experimental.pallas import tpu as pltpu
from jax.sharding import PartitionSpec as P

ITERS = 2
CHUNKS = 8
MESH = pl.DeviceIdType.MESH
SCHEDULE = (
    (((0, -1, 3), (0, -1, 2), (0, 0, 0), (0, 0, 1), (0, 0, 2), (0, 1, 1), (0, 1, 0), (0, 0, 3), (0, 2, 0), (0, 2, 1), (0, 1, 2), (0, 1, 3), (0, 3, 0),),
     ((0, 0, 1), (0, 0, 0), (0, 1, 1), (0, -1, 2), (0, 1, 0), (0, 2, 1), (0, 2, 0), (0, 3, 0), (0, 0, 2), (0, -1, 3),),
     ("spread", 0)),
    (((0, 3, 1),),
     ((0, 3, 1),),
     ("spread", 1)),
    ((),
     (),
     ("out",)),
    (((0, 2, 2), (0, 2, 3), (0, 3, 2),),
     ((0, 1, 2), (0, 0, 3), (0, 2, 2), (0, 1, 3), (0, 3, 2),),
     ("spread", 2)),
    ((),
     (),
     ("in",)),
    ((),
     ((0, 2, 3),),
     ("edge",)),
    ((),
     (),
     ("early",)),
    (((0, 3, 3),),
     ((0, 3, 3),),
     ("spread", 3)),
    ((),
     (),
     ("late", 1)),
    ((),
     (),
     ("late", 2)),
    ((),
     (),
     ("correct", 3)),
    ((),
     (),
     ("correct", 2)),
    (((1, 0, 3),),
     (),
     ("near",)),
    ((),
     (),
     ("correct", 1)),
    (((1, 0, 2), (1, 1, 3), (1, 0, 1),),
     (),
     ("correct", 0)),
    (((1, 1, 2), (1, 1, 1), (1, 0, 0), (1, 1, 0), (1, 2, 3), (1, 2, 1), (1, 2, 2), (1, 2, 0), (1, 3, 1), (1, 3, 2), (1, 3, 0), (1, 3, 3),),
     ((1, 0, 1), (1, 0, 3), (1, 0, 0), (1, 0, 2), (1, 1, 1), (1, 1, 3), (1, 1, 0), (1, 2, 1), (1, 1, 2), (1, 2, 2), (1, 2, 3), (1, 2, 0), (1, 3, 3), (1, 3, 2), (1, 3, 0), (1, 3, 1),),
     None),
)
F32, BF16 = jnp.float32, jnp.bfloat16


def split(value):
    high = value.astype(BF16)
    return high, (value - high.astype(F32)).astype(BF16)


def band(taps, row, size, row_sign, scale):
    rows = lax.broadcasted_iota(jnp.int32, (size, size), 0)
    cols = lax.broadcasted_iota(jnp.int32, (size, size), 1)
    count = taps.shape[2]
    offset = (cols - rows) * row_sign + (count - 1) // 2
    total = jnp.zeros((size, size), F32)
    for k in range(count):
        total = jnp.where(offset == k, taps[row, 0, k], total)
    return split(total * scale)


def kernel(dims, taps, est_in, seen_in, mask_in, out,
           est, ext, seen, mask, wsum, nums, recvs, xbuf, ymats, zmats,
           mask_sem, load_sem, halo_send, halo_recv, rs_send, rs_recv, ag_send, ag_recv):
    views, blks, bits = dims
    slab, cy, cz = seen.shape
    count = taps.shape[2]
    rad = (count - 1) // 2
    chunks = CHUNKS
    chunk = slab // chunks
    half = chunks // 2
    order = [t // 2 if t % 2 == 0 else chunks - 1 - t // 2 for t in range(chunks)]
    turn = [order.index(c) % bits for c in range(chunks)]
    v, b = lax.axis_index("view"), lax.axis_index("blk")
    bit = [(v // 2**p) % 2 for p in range(bits)]
    partner = [v + (1 - 2 * bit[p]) * 2**p for p in range(bits)]
    left, right = (b + blks - 1) % blks, (b + 1) % blks

    def planes(p):
        return pl.ds(p * chunk, chunk)

    mask_loads = [
        pltpu.make_async_copy(mask_in.at[0, planes(p)], mask.at[planes(p)], mask_sem.at[p])
        for p in range(chunks)
    ]
    loads = [
        pltpu.make_async_copy(est_in, ext.at[0, pl.ds(rad, slab)], load_sem.at[0]),
        pltpu.make_async_copy(seen_in.at[0], seen, load_sem.at[1]),
    ]
    for p in order:
        mask_loads[p].start()
    for load in loads:
        load.start()

    barrier = pltpu.get_barrier_semaphore()
    for p in range(bits):
        pl.semaphore_signal(barrier, inc=1, device_id=(partner[p], b), device_id_type=MESH)
    for near in (left, right):
        pl.semaphore_signal(barrier, inc=1, device_id=(v, near), device_id_type=MESH)

    def halo(which, side, part):
        cut = chunk if which else rad - chunk
        reach, size = ((0, cut), (cut, rad - cut))[part]
        start, land, near = (
            (slab - reach - size, rad - reach - size, right), (reach, rad + slab + reach, left))[side]
        src = ext.at[which, pl.ds(rad + start, size)] if which else est_in.at[pl.ds(start, size)]
        return pltpu.make_async_remote_copy(
            src_ref=src, dst_ref=ext.at[which, pl.ds(land, size)],
            send_sem=halo_send.at[which, side, part], recv_sem=halo_recv.at[which, side, part],
            device_id=(v, near), device_id_type=MESH)

    def halo_start(which, part):
        @pl.when(b < blks - 1)
        def _():
            halo(which, 0, part).start()

        @pl.when(b > 0)
        def _():
            halo(which, 1, part).start()

    def halo_wait(which, part):
        @pl.when(b > 0)
        def _():
            halo(which, 0, part).wait_recv()

        @pl.when(b < blks - 1)
        def _():
            halo(which, 1, part).wait_recv()

    def no_neighbour(which):
        @pl.when(b == 0)
        def _():
            ext[which, pl.ds(0, rad)] = jnp.zeros((rad, cy, cz), F32)

        @pl.when(b == blks - 1)
        def _():
            ext[which, pl.ds(rad + slab, rad)] = jnp.zeros((rad, cy, cz), F32)

    def halo_sent(which):
        for part in range(2):
            @pl.when(b < blks - 1)
            def _():
                halo(which, 0, part).wait_send()

            @pl.when(b > 0)
            def _():
                halo(which, 1, part).wait_send()

    def way(p, s):
        return (turn[p] + s) % bits

    def region(p, s):
        start, length = 0, cy
        for t in range(s):
            length //= 2
            start = start + bit[way(p, t)] * length
        return start, length

    def lines(start, length):
        if not isinstance(start, int):
            start = pl.multiple_of(start, 8)
        return pl.ds(start, length)

    def rs_copy(r, s, p):
        buf = wsum if r == 0 else nums.at[r - 1]
        start, length = region(p, s)
        length //= 2
        mine = bit[way(p, s)]
        return pltpu.make_async_remote_copy(
            src_ref=buf.at[planes(p), lines(start + (1 - mine) * length, length)],
            dst_ref=recvs.at[r, planes(p), pl.ds(cy - cy // 2**s, length)],
            send_sem=rs_send.at[r, s, p], recv_sem=rs_recv.at[r, s, p],
            device_id=(partner[way(p, s)], b), device_id_type=MESH)

    def rs_take(r, s, p):
        buf = wsum if r == 0 else nums.at[r - 1]
        rs_copy(r, s, p).wait_recv()
        start, length = region(p, s + 1)
        kept, came = lines(start, length), pl.ds(cy - cy // 2**s, length)

        def add(i, carry):
            cell = p * chunk + i
            buf[cell, kept] = buf[cell, kept] + recvs[r, cell, came]
            return carry

        lax.fori_loop(0, chunk, add, 0)

    def ag_copy(r, s, p):
        start, length = region(p, s + 1)
        if r < ITERS - 1:
            ref = est.at[r, planes(p), lines(start, length)]
        else:
            ref = out.at[planes(p), lines(start, length)]
        return pltpu.make_async_remote_copy(
            src_ref=ref, dst_ref=ref,
            send_sem=ag_send.at[r, s, p], recv_sem=ag_recv.at[r, s, p],
            device_id=(partner[way(p, s)], b), device_id_type=MESH)

    def windows(step):
        height = 8

        def run(j, carry):
            step((pl.ds(pl.multiple_of(j * height, height), height), slice(None)))
            return carry

        lax.fori_loop(0, cy // height, run, 0)

    def sweep(which, first, window, back, keep=None):
        totals = [None] * chunk
        for k in range(count + chunk - 1):
            if keep is not None and not keep(k):
                continue
            plane = ext[(which, first + k) + window]
            for i in range(max(0, k - count + 1), min(chunk, k + 1)):
                tap = k - i
                term = taps[0, 0, count - 1 - tap if back else tap] * plane
                totals[i] = term if totals[i] is None else totals[i] + term
        return totals

    def in_plane(cells, back):
        blurred = []
        for cell in cells:
            high, low = split(cell)
            stack = jnp.concatenate([high, high, low], axis=0)
            blurred.append(jnp.dot(ymats[back], stack, preferred_element_type=F32))
        high, low = split(jnp.concatenate(blurred, axis=0))
        high_mat, low_mat = zmats[back, 0], zmats[back, 1]
        result = jnp.dot(high, high_mat, preferred_element_type=F32)
        result += jnp.dot(low, high_mat, preferred_element_type=F32)
        result += jnp.dot(high, low_mat, preferred_element_type=F32)
        result = result.reshape(2, chunk, cy, cz)
        return result[0], result[1]

    def pair(t):
        return t, chunks - 1 - t

    def blur(which, t, back):
        for side, c in enumerate(pair(t)):
            def rows(window, side=side, c=c):
                totals = sweep(which, c * chunk, window, back)
                for i in range(chunk):
                    xbuf[(side * chunk + i,) + window] = totals[i]

            windows(rows)
        return in_plane([xbuf[i] for i in range(2 * chunk)], back)

    def over(step, first, last, inward=True):
        def run(t, carry):
            step(t if inward else half - 1 - t)
            return carry

        lax.fori_loop(first, last, run, 0)

    for p in order[:2]:
        mask_loads[p].wait()

        def to_float(i, carry):
            wsum[p * chunk + i] = mask[p * chunk + i].astype(F32)
            return carry

        lax.fori_loop(0, chunk, to_float, 0)

    pl.semaphore_wait(barrier, bits + 2)
    for p in order[:2]:
        rs_copy(0, 0, p).start()
    for part in range(2):
        halo_start(0, part)
    for p in order[2:]:
        mask_loads[p].wait()

        def to_float(i, carry):
            wsum[p * chunk + i] = mask[p * chunk + i].astype(F32)
            return carry

        lax.fori_loop(0, chunk, to_float, 0)
        rs_copy(0, 0, p).start()

    for which in range(2 * ITERS):
        no_neighbour(which)

    sums = []
    for row in range(3):
        total = taps[row, 0, 0]
        for k in range(1, count):
            total = total + taps[row, 0, k]
        sums.append(jnp.full((1, cz), total, F32))
    y_scale = (1.0 / (sums[0] * sums[1]))[:, :cy]
    z_scale = 1.0 / sums[2]
    for back in range(2):
        sign = -1 if back else 1
        high, low = band(taps, 1, cy, sign, y_scale)
        ymats[back] = jnp.concatenate([high, low, high], axis=1)
        high, low = band(taps, 2, cz, -sign, z_scale)
        zmats[back, 0] = high
        zmats[back, 1] = low
    for load in loads:
        load.wait()

    def quotient(t):
        for c, blurred in zip(pair(t), blur(0, t, 0)):
            ext[1, pl.ds(rad + c * chunk, chunk)] = seen[planes(c)] / blurred

    def spread(r):
        def step(t):
            cells = [est[r - 1, c * chunk + i] for c in pair(t) for i in range(chunk)]
            for c, blurred in zip(pair(t), in_plane(cells, 0)):
                ext[2 * r, pl.ds(rad + c * chunk, chunk)] = blurred

        return step

    low_last, high_last = (half - 1) * chunk, (half + 1) * chunk

    def divide(r, c, part):
        def late(k):
            return low_last <= c * chunk + k - rad < high_last

        keep = {"all": None, "early": lambda k: not late(k), "late": late}[part]

        def rows(window):
            totals = sweep(2 * r, c * chunk, window, 0, keep)
            for i in range(chunk):
                cell = c * chunk + i
                place = (2 * r + 1, rad + cell) + window
                total = totals[i]
                if part == "late":
                    total = ext[place] if total is None else ext[place] + total
                elif total is None:
                    total = jnp.zeros((8, cz), F32)
                ext[place] = total if part == "early" else seen[(cell,) + window] / total

        windows(rows)

    def correct(r, send):
        def step(t):
            for c, corrected in zip(pair(t), blur(2 * r + 1, t, 1)):
                nums[r, planes(c)] = mask[planes(c)].astype(F32) * corrected
            if send:
                for u in range(half):
                    @pl.when(t == u)
                    def _(u=u):
                        for p in pair(u):
                            rs_copy(r + 1, 0, p).start()

        return step

    def update(r, p):
        start, length = region(p, bits)
        kept = lines(start, length)

        def cells(i, carry):
            cell = p * chunk + i
            old = est[r - 1, cell, kept] if r else ext[0, rad + cell, kept]
            fresh = old * nums[r, cell, kept] / wsum[cell, kept]
            if r < ITERS - 1:
                est[r, cell, kept] = fresh
            else:
                out[cell, kept] = fresh
            return carry

        lax.fori_loop(0, chunk, cells, 0)

    def event(r, e, p):
        if e < bits:
            rs_take(r + 1, e, p)
            if e + 1 < bits:
                rs_copy(r + 1, e + 1, p).start()
            else:
                update(r, p)
                ag_copy(r, bits - 1, p).start()
        else:
            s = 2 * bits - 1 - e
            ag_copy(r, s, p).wait_recv()
            if s > 0:
                ag_copy(r, s - 1, p).start()

    over(quotient, 2, half)
    halo_wait(0, 0)
    over(quotient, 1, 2)
    halo_start(1, 1)
    halo_wait(0, 1)
    over(quotient, 0, 1)
    halo_start(1, 0)
    over(correct(0, False), 0, half - 2, inward=False)
    for p in order:
        rs_take(0, 0, p)
        if bits > 1:
            rs_copy(0, 1, p).start()
    for part in range(2):
        halo_wait(1, part)
    over(correct(0, True), 0, 2)
    for s in range(1, bits):
        for p in order:
            rs_take(0, s, p)
            if s + 1 < bits:
                rs_copy(0, s + 1, p).start()

    def step(r, stage, t):
        for p in pair(t):
            if stage < 0:
                rs_copy(r + 1, 0, p).start()
                continue
            stages = ((0,), range(1, bits), range(bits, 2 * bits - 1), (2 * bits - 1,))[stage]
            for e in stages:
                event(r, e, p)

    def compute(kind, t=0):
        if kind == "spread":
            over(spread(1), t, t + 1)
        elif kind == "out":
            for part in range(2):
                halo_start(2, part)
        elif kind == "in":
            for part in range(2):
                halo_wait(2, part)
        elif kind == "edge":
            for c in pair(0):
                divide(1, c, "all")
            halo_start(3, 0)
        elif kind == "early":
            for u in range(1, half):
                for c in pair(u):
                    divide(1, c, "early")
        elif kind == "late":
            for u in range(t, 2 if t == 1 else half):
                for c in pair(u):
                    divide(1, c, "late")
            if t == 1:
                halo_start(3, 1)
        elif kind == "correct":
            over(correct(1, True), half - 1 - t, half - t, inward=False)
        elif kind == "near":
            for part in range(2):
                halo_wait(3, part)

    for even, odd, work in SCHEDULE:
        if even == odd:
            for item in even:
                step(*item)
        else:
            for parity, items in enumerate((even, odd)):
                @pl.when(b % 2 == parity)
                def _(items=items):
                    for item in items:
                        step(*item)
        if work:
            compute(*work)

    for which in range(2 * ITERS):
        halo_sent(which)
    for s in range(bits):
        for p in range(chunks):
            for r in range(ITERS + 1):
                rs_copy(r, s, p).wait_send()
            for r in range(ITERS):
                ag_copy(r, s, p).wait_send()


def body(views, blks, estimate, views_seen, weight_mask, psf):
    slab, cy, cz = estimate.shape
    bits = views.bit_length() - 1
    hbm = pl.BlockSpec(memory_space=pl.ANY)
    vmem = pltpu.VMEM
    dma = pltpu.SemaphoreType.DMA
    count = psf.shape[-1]
    rad = (count - 1) // 2
    chunks = CHUNKS
    return pl.pallas_call(
        functools.partial(kernel, (views, blks, bits)),
        out_shape=vmem(estimate.shape, F32),
        in_specs=[pl.BlockSpec(memory_space=pltpu.SMEM), hbm, hbm, hbm],
        out_specs=pl.BlockSpec(memory_space=vmem),
        scratch_shapes=[
            vmem((ITERS - 1, slab, cy, cz), F32),
            vmem((2 * ITERS, slab + 2 * rad, cy, cz), F32),
            vmem((slab, cy, cz), F32),
            vmem((slab, cy, cz), jnp.int32),
            vmem((slab, cy, cz), F32),
            vmem((ITERS, slab, cy, cz), F32),
            vmem((ITERS + 1, slab, cy - cy // views, cz), F32),
            vmem((2 * (slab // chunks), cy, cz), F32),
            vmem((2, cy, 3 * cy), BF16),
            vmem((2, 2, cz, cz), BF16),
            dma((chunks,)),
            dma((2,)),
            dma((2 * ITERS, 2, 2)),
            dma((2 * ITERS, 2, 2)),
            dma((ITERS + 1, bits, chunks)),
            dma((ITERS + 1, bits, chunks)),
            dma((ITERS, bits, chunks)),
            dma((ITERS, bits, chunks)),
        ],
        compiler_params=pltpu.CompilerParams(
            collective_id=0, has_side_effects=True, vmem_limit_bytes=56 * 2**20),
    )(jnp.transpose(psf, (1, 0, 2)), estimate, views_seen, weight_mask)


def solution(mesh):
    placed = (
        P("blk", None, None),
        P("view", "blk", None, None),
        P("view", "blk", None, None),
        P("view", None, None),
    )
    return jax.shard_map(
        functools.partial(body, mesh.shape["view"], mesh.shape["blk"]),
        mesh=mesh, in_specs=placed, out_specs=P("blk", None, None), check_vma=False
    )
```

```python
import functools

import jax
import jax.numpy as jnp
from jax import lax
from jax.experimental import pallas as pl
from jax.experimental.pallas import tpu as pltpu
from jax.sharding import PartitionSpec as P

ITERS = 2
CHUNKS = 8
MESH = pl.DeviceIdType.MESH
SCHEDULE = (
    (((0, -1, 2), (0, 0, 0), (0, 0, 1), (0, 1, 0), (0, 1, 1), (0, -1, 3), (0, 2, 0), (0, 0, 2), (0, 0, 3), (0, 1, 2), (0, 3, 0), (0, 2, 1),),
     ((0, 0, 0), (0, 1, 0), (0, 0, 1), (0, -1, 2), (0, 2, 0), (0, 1, 1), (0, 2, 1), (0, 0, 2), (0, 3, 0),),
     ("spread", 0)),
    (((0, 1, 3), (0, 2, 2), (0, 3, 1),),
     ((0, 3, 1),),
     ("spread", 1)),
    (((0, 2, 3),),
     (),
     ("out",)),
    (((0, 3, 2),),
     ((0, -1, 3), (0, 1, 2), (0, 0, 3), (0, 2, 2), (0, 1, 3), (0, 3, 2),),
     ("spread", 2)),
    ((),
     (),
     ("in",)),
    ((),
     ((0, 2, 3),),
     ("edge",)),
    ((),
     (),
     ("early",)),
    (((0, 3, 3),),
     ((0, 3, 3),),
     ("spread", 3)),
    ((),
     (),
     ("late", 1)),
    ((),
     (),
     ("late", 2)),
    ((),
     (),
     ("correct", 3)),
    ((),
     (),
     ("correct", 2)),
    (((1, 0, 3),),
     ((1, 0, 3),),
     ("near",)),
    ((),
     (),
     ("correct", 1)),
    (((1, 0, 2), (1, 1, 2), (1, 1, 3),),
     (),
     ("correct", 0)),
    (((1, 2, 2), (1, 2, 3), (1, 0, 0), (1, 0, 1), (1, 1, 0), (1, 1, 1), (1, 2, 0), (1, 2, 1), (1, 3, 1), (1, 3, 0), (1, 3, 2), (1, 3, 3),),
     ((1, 0, 2), (1, 0, 1), (1, 1, 2), (1, 0, 0), (1, 1, 3), (1, 1, 1), (1, 1, 0), (1, 2, 2), (1, 2, 0), (1, 2, 1), (1, 2, 3), (1, 3, 2), (1, 3, 3), (1, 3, 1), (1, 3, 0),),
     None),
)
F32, BF16 = jnp.float32, jnp.bfloat16


def split(value):
    high = value.astype(BF16)
    return high, (value - high.astype(F32)).astype(BF16)


def band(taps, row, size, row_sign, scale):
    rows = lax.broadcasted_iota(jnp.int32, (size, size), 0)
    cols = lax.broadcasted_iota(jnp.int32, (size, size), 1)
    count = taps.shape[2]
    offset = (cols - rows) * row_sign + (count - 1) // 2
    total = jnp.zeros((size, size), F32)
    for k in range(count):
        total = jnp.where(offset == k, taps[row, 0, k], total)
    return split(total * scale)


def kernel(dims, taps, est_in, seen_in, mask_in, out,
           est, ext, seen, mask, wsum, nums, recvs, xbuf, ymats, zmats,
           mask_sem, load_sem, halo_send, halo_recv, rs_send, rs_recv, ag_send, ag_recv):
    views, blks, bits = dims
    slab, cy, cz = seen.shape
    count = taps.shape[2]
    rad = (count - 1) // 2
    chunks = CHUNKS
    chunk = slab // chunks
    half = chunks // 2
    order = [t // 2 if t % 2 == 0 else chunks - 1 - t // 2 for t in range(chunks)]
    turn = [order.index(c) % bits for c in range(chunks)]
    v, b = lax.axis_index("view"), lax.axis_index("blk")
    bit = [(v // 2**p) % 2 for p in range(bits)]
    partner = [v + (1 - 2 * bit[p]) * 2**p for p in range(bits)]
    left, right = (b + blks - 1) % blks, (b + 1) % blks

    def planes(p):
        return pl.ds(p * chunk, chunk)

    mask_loads = [
        pltpu.make_async_copy(mask_in.at[0, planes(p)], mask.at[planes(p)], mask_sem.at[p])
        for p in range(chunks)
    ]
    loads = [
        pltpu.make_async_copy(est_in, ext.at[0, pl.ds(rad, slab)], load_sem.at[0]),
        pltpu.make_async_copy(seen_in.at[0], seen, load_sem.at[1]),
    ]
    for p in order:
        mask_loads[p].start()
    for load in loads:
        load.start()

    barrier = pltpu.get_barrier_semaphore()
    for p in range(bits):
        pl.semaphore_signal(barrier, inc=1, device_id=(partner[p], b), device_id_type=MESH)
    for near in (left, right):
        pl.semaphore_signal(barrier, inc=1, device_id=(v, near), device_id_type=MESH)

    def halo(which, side, part):
        cut = chunk if which else rad - chunk
        reach, size = ((0, cut), (cut, rad - cut))[part]
        start, land, near = (
            (slab - reach - size, rad - reach - size, right), (reach, rad + slab + reach, left))[side]
        src = ext.at[which, pl.ds(rad + start, size)] if which else est_in.at[pl.ds(start, size)]
        return pltpu.make_async_remote_copy(
            src_ref=src, dst_ref=ext.at[which, pl.ds(land, size)],
            send_sem=halo_send.at[which, side, part], recv_sem=halo_recv.at[which, side, part],
            device_id=(v, near), device_id_type=MESH)

    def halo_start(which, part):
        @pl.when(b < blks - 1)
        def _():
            halo(which, 0, part).start()

        @pl.when(b > 0)
        def _():
            halo(which, 1, part).start()

    def halo_wait(which, part):
        @pl.when(b > 0)
        def _():
            halo(which, 0, part).wait_recv()

        @pl.when(b < blks - 1)
        def _():
            halo(which, 1, part).wait_recv()

    def no_neighbour(which):
        @pl.when(b == 0)
        def _():
            ext[which, pl.ds(0, rad)] = jnp.zeros((rad, cy, cz), F32)

        @pl.when(b == blks - 1)
        def _():
            ext[which, pl.ds(rad + slab, rad)] = jnp.zeros((rad, cy, cz), F32)

    def halo_sent(which):
        for part in range(2):
            @pl.when(b < blks - 1)
            def _():
                halo(which, 0, part).wait_send()

            @pl.when(b > 0)
            def _():
                halo(which, 1, part).wait_send()

    def way(p, s):
        return (turn[p] + s) % bits

    def region(p, s):
        start, length = 0, cy
        for t in range(s):
            length //= 2
            start = start + bit[way(p, t)] * length
        return start, length

    def lines(start, length):
        if not isinstance(start, int):
            start = pl.multiple_of(start, 8)
        return pl.ds(start, length)

    def rs_copy(r, s, p):
        buf = wsum if r == 0 else nums.at[r - 1]
        start, length = region(p, s)
        length //= 2
        mine = bit[way(p, s)]
        return pltpu.make_async_remote_copy(
            src_ref=buf.at[planes(p), lines(start + (1 - mine) * length, length)],
            dst_ref=recvs.at[r, planes(p), pl.ds(cy - cy // 2**s, length)],
            send_sem=rs_send.at[r, s, p], recv_sem=rs_recv.at[r, s, p],
            device_id=(partner[way(p, s)], b), device_id_type=MESH)

    def rs_take(r, s, p):
        buf = wsum if r == 0 else nums.at[r - 1]
        rs_copy(r, s, p).wait_recv()
        start, length = region(p, s + 1)
        kept, came = lines(start, length), pl.ds(cy - cy // 2**s, length)

        def add(i, carry):
            cell = p * chunk + i
            buf[cell, kept] = buf[cell, kept] + recvs[r, cell, came]
            return carry

        lax.fori_loop(0, chunk, add, 0)

    def ag_copy(r, s, p):
        start, length = region(p, s + 1)
        if r < ITERS - 1:
            ref = est.at[r, planes(p), lines(start, length)]
        else:
            ref = out.at[planes(p), lines(start, length)]
        return pltpu.make_async_remote_copy(
            src_ref=ref, dst_ref=ref,
            send_sem=ag_send.at[r, s, p], recv_sem=ag_recv.at[r, s, p],
            device_id=(partner[way(p, s)], b), device_id_type=MESH)

    def windows(step):
        height = 8

        def run(j, carry):
            step((pl.ds(pl.multiple_of(j * height, height), height), slice(None)))
            return carry

        lax.fori_loop(0, cy // height, run, 0)

    def sweep(which, first, window, back, keep=None):
        totals = [None] * chunk
        for k in range(count + chunk - 1):
            if keep is not None and not keep(k):
                continue
            plane = ext[(which, first + k) + window]
            for i in range(max(0, k - count + 1), min(chunk, k + 1)):
                tap = k - i
                term = taps[0, 0, count - 1 - tap if back else tap] * plane
                totals[i] = term if totals[i] is None else totals[i] + term
        return totals

    def in_plane(cells, back):
        blurred = []
        for cell in cells:
            high, low = split(cell)
            stack = jnp.concatenate([high, high, low], axis=0)
            blurred.append(jnp.dot(ymats[back], stack, preferred_element_type=F32))
        high, low = split(jnp.concatenate(blurred, axis=0))
        high_mat, low_mat = zmats[back, 0], zmats[back, 1]
        result = jnp.dot(high, high_mat, preferred_element_type=F32)
        result += jnp.dot(low, high_mat, preferred_element_type=F32)
        result += jnp.dot(high, low_mat, preferred_element_type=F32)
        result = result.reshape(2, chunk, cy, cz)
        return result[0], result[1]

    def pair(t):
        return t, chunks - 1 - t

    def blur(which, t, back):
        for side, c in enumerate(pair(t)):
            def rows(window, side=side, c=c):
                totals = sweep(which, c * chunk, window, back)
                for i in range(chunk):
                    xbuf[(side * chunk + i,) + window] = totals[i]

            windows(rows)
        return in_plane([xbuf[i] for i in range(2 * chunk)], back)

    for p in order[:2]:
        mask_loads[p].wait()

        def to_float(i, carry):
            wsum[p * chunk + i] = mask[p * chunk + i].astype(F32)
            return carry

        lax.fori_loop(0, chunk, to_float, 0)

    pl.semaphore_wait(barrier, bits + 2)
    for p in order[:2]:
        rs_copy(0, 0, p).start()
    for part in range(2):
        halo_start(0, part)
    for p in order[2:]:
        mask_loads[p].wait()

        def to_float(i, carry):
            wsum[p * chunk + i] = mask[p * chunk + i].astype(F32)
            return carry

        lax.fori_loop(0, chunk, to_float, 0)
        rs_copy(0, 0, p).start()

    for which in range(2 * ITERS):
        no_neighbour(which)

    sums = []
    for row in range(3):
        total = taps[row, 0, 0]
        for k in range(1, count):
            total = total + taps[row, 0, k]
        sums.append(jnp.full((1, cz), total, F32))
    y_scale = (1.0 / (sums[0] * sums[1]))[:, :cy]
    z_scale = 1.0 / sums[2]
    for back in range(2):
        sign = -1 if back else 1
        high, low = band(taps, 1, cy, sign, y_scale)
        ymats[back] = jnp.concatenate([high, low, high], axis=1)
        high, low = band(taps, 2, cz, -sign, z_scale)
        zmats[back, 0] = high
        zmats[back, 1] = low
    for load in loads:
        load.wait()

    def quotient(t):
        for c, blurred in zip(pair(t), blur(0, t, 0)):
            ext[1, pl.ds(rad + c * chunk, chunk)] = seen[planes(c)] / blurred

    def spread(r):
        def step(t):
            cells = [est[r - 1, c * chunk + i] for c in pair(t) for i in range(chunk)]
            for c, blurred in zip(pair(t), in_plane(cells, 0)):
                ext[2 * r, pl.ds(rad + c * chunk, chunk)] = blurred

        return step

    low_last, high_last = (half - 1) * chunk, (half + 1) * chunk

    def divide(r, c, part):
        def late(k):
            return low_last <= c * chunk + k - rad < high_last

        keep = {"all": None, "early": lambda k: not late(k), "late": late}[part]

        def rows(window):
            totals = sweep(2 * r, c * chunk, window, 0, keep)
            for i in range(chunk):
                cell = c * chunk + i
                place = (2 * r + 1, rad + cell) + window
                total = totals[i]
                if part == "late":
                    total = ext[place] if total is None else ext[place] + total
                elif total is None:
                    total = jnp.zeros((8, cz), F32)
                ext[place] = total if part == "early" else seen[(cell,) + window] / total

        windows(rows)

    def correct(r, send):
        def step(t):
            for c, corrected in zip(pair(t), blur(2 * r + 1, t, 1)):
                nums[r, planes(c)] = mask[planes(c)].astype(F32) * corrected
            if send:
                for u in range(send):
                    @pl.when(t == u)
                    def _(u=u):
                        for p in pair(u):
                            rs_copy(r + 1, 0, p).start()

        return step

    def update(r, p):
        start, length = region(p, bits)
        kept = lines(start, length)

        def cells(i, carry):
            cell = p * chunk + i
            old = est[r - 1, cell, kept] if r else ext[0, rad + cell, kept]
            fresh = old * nums[r, cell, kept] / wsum[cell, kept]
            if r < ITERS - 1:
                est[r, cell, kept] = fresh
            else:
                out[cell, kept] = fresh
            return carry

        lax.fori_loop(0, chunk, cells, 0)

    def event(r, e, p):
        if e < bits:
            rs_take(r + 1, e, p)
            if e + 1 < bits:
                rs_copy(r + 1, e + 1, p).start()
            else:
                update(r, p)
                ag_copy(r, bits - 1, p).start()
        else:
            s = 2 * bits - 1 - e
            ag_copy(r, s, p).wait_recv()
            if s > 0:
                ag_copy(r, s - 1, p).start()

    def ordered(work, turns, before):
        def run(u, carry):
            for k in range(half):
                if k in before:
                    pl.when(u == k)(before[k])
            t = turns[0]
            for k in range(1, half):
                t = jnp.where(u == k, turns[k], t)
            work(t)
            return carry

        lax.fori_loop(0, half, run, 0)

    def near_came():
        halo_wait(0, 0)

    def far_came():
        halo_start(1, 1)
        halo_wait(0, 1)

    def weights_came():
        for p in order:
            rs_take(0, 0, p)
            if bits > 1:
                rs_copy(0, 1, p).start()
        for part in range(2):
            halo_wait(1, part)

    ordered(quotient, [*range(2, half), 1, 0], {half - 2: near_came, half - 1: far_came})
    halo_start(1, 0)
    ordered(correct(0, 2), [*range(half - 1, 1, -1), 0, 1], {half - 2: weights_came})
    for s in range(1, bits):
        for p in order:
            rs_take(0, s, p)
            if s + 1 < bits:
                rs_copy(0, s + 1, p).start()

    def step(r, stage, t):
        for p in pair(t):
            if stage < 0:
                rs_copy(r + 1, 0, p).start()
                continue
            stages = ((0,), range(1, bits), range(bits, 2 * bits - 1), (2 * bits - 1,))[stage]
            for e in stages:
                event(r, e, p)

    def compute(kind, t=0):
        if kind == "out":
            for part in range(2):
                halo_start(2, part)
        elif kind == "in":
            for part in range(2):
                halo_wait(2, part)
        elif kind == "edge":
            for c in pair(0):
                divide(1, c, "all")
            halo_start(3, 0)
        elif kind == "early":
            for u in range(1, half):
                for c in pair(u):
                    divide(1, c, "early")
        elif kind == "late":
            for u in range(t, 2 if t == 1 else half):
                for c in pair(u):
                    divide(1, c, "late")
            if t == 1:
                halo_start(3, 1)
        elif kind == "near":
            for part in range(2):
                halo_wait(3, part)

    def entry(even, odd, work):
        if even == odd:
            for item in even:
                step(*item)
        else:
            for parity, items in enumerate((even, odd)):
                @pl.when(b % 2 == parity)
                def _(items=items):
                    for item in items:
                        step(*item)
        if work and work[0] not in ("spread", "correct"):
            compute(*work)

    def entries(rows):
        def emit():
            for row in rows:
                entry(*row)

        return emit

    def looped(kind, rows, work):
        ends = [k for k, row in enumerate(rows) if row[2] and row[2][0] == kind]
        before, start = {}, 0
        for u, end in enumerate(ends):
            part = rows[start:end + 1]
            if any(row[0] or row[1] or row[2][0] != kind for row in part):
                before[u] = entries(part)
            start = end + 1
        ordered(work, [rows[k][2][1] for k in ends], before)
        return rows[start:]

    rows = looped("spread", list(SCHEDULE), spread(1))
    for k in range(len(rows)):
        if rows[k][2][0] == "correct":
            break
        entry(*rows[k])
    rows = looped("correct", rows[k:], correct(1, half))
    entries(rows)()

    for which in range(2 * ITERS):
        halo_sent(which)
    for s in range(bits):
        for p in range(chunks):
            for r in range(ITERS + 1):
                rs_copy(r, s, p).wait_send()
            for r in range(ITERS):
                ag_copy(r, s, p).wait_send()


def body(views, blks, estimate, views_seen, weight_mask, psf):
    slab, cy, cz = estimate.shape
    bits = views.bit_length() - 1
    hbm = pl.BlockSpec(memory_space=pl.ANY)
    vmem = pltpu.VMEM
    dma = pltpu.SemaphoreType.DMA
    count = psf.shape[-1]
    rad = (count - 1) // 2
    chunks = CHUNKS
    return pl.pallas_call(
        functools.partial(kernel, (views, blks, bits)),
        out_shape=vmem(estimate.shape, F32),
        in_specs=[pl.BlockSpec(memory_space=pltpu.SMEM), hbm, hbm, hbm],
        out_specs=pl.BlockSpec(memory_space=vmem),
        scratch_shapes=[
            vmem((ITERS - 1, slab, cy, cz), F32),
            vmem((2 * ITERS, slab + 2 * rad, cy, cz), F32),
            vmem((slab, cy, cz), F32),
            vmem((slab, cy, cz), jnp.int32),
            vmem((slab, cy, cz), F32),
            vmem((ITERS, slab, cy, cz), F32),
            vmem((ITERS + 1, slab, cy - cy // views, cz), F32),
            vmem((2 * (slab // chunks), cy, cz), F32),
            vmem((2, cy, 3 * cy), BF16),
            vmem((2, 2, cz, cz), BF16),
            dma((chunks,)),
            dma((2,)),
            dma((2 * ITERS, 2, 2)),
            dma((2 * ITERS, 2, 2)),
            dma((ITERS + 1, bits, chunks)),
            dma((ITERS + 1, bits, chunks)),
            dma((ITERS, bits, chunks)),
            dma((ITERS, bits, chunks)),
        ],
        compiler_params=pltpu.CompilerParams(
            collective_id=0, has_side_effects=True, vmem_limit_bytes=56 * 2**20),
    )(jnp.transpose(psf, (1, 0, 2)), estimate, views_seen, weight_mask)


def solution(mesh):
    placed = (
        P("blk", None, None),
        P("view", "blk", None, None),
        P("view", "blk", None, None),
        P("view", None, None),
    )
    return jax.shard_map(
        functools.partial(body, mesh.shape["view"], mesh.shape["blk"]),
        mesh=mesh, in_specs=placed, out_specs=P("blk", None, None), check_vma=False
    )
```

```python
import functools

import jax
import jax.numpy as jnp
from jax import lax
from jax.experimental import pallas as pl
from jax.experimental.pallas import tpu as pltpu
from jax.sharding import PartitionSpec as P

ITERS = 2
CHUNKS = 8
MESH = pl.DeviceIdType.MESH
SCHEDULE = (
    (((0, -1, 2), (0, 0, 0), (0, 0, 1), (0, 1, 0), (0, 1, 1), (0, -1, 3), (0, 2, 0), (0, 0, 2), (0, 0, 3), (0, 1, 2), (0, 3, 0), (0, 2, 1),),
     ((0, 0, 0), (0, 1, 0), (0, 0, 1), (0, -1, 2), (0, 2, 0), (0, 1, 1), (0, 2, 1), (0, 0, 2), (0, 3, 0),),
     ("spread", 0)),
    (((0, 1, 3), (0, 2, 2), (0, 3, 1),),
     ((0, 3, 1),),
     ("spread", 1)),
    (((0, 2, 3),),
     (),
     ("out",)),
    (((0, 3, 2),),
     ((0, -1, 3), (0, 1, 2), (0, 0, 3), (0, 2, 2), (0, 1, 3), (0, 3, 2),),
     ("spread", 2)),
    ((),
     (),
     ("in",)),
    ((),
     ((0, 2, 3),),
     ("edge",)),
    ((),
     (),
     ("early",)),
    (((0, 3, 3),),
     ((0, 3, 3),),
     ("spread", 3)),
    ((),
     (),
     ("late", 1)),
    ((),
     (),
     ("late", 2)),
    ((),
     (),
     ("correct", 3)),
    ((),
     (),
     ("correct", 2)),
    (((1, 0, 3),),
     ((1, 0, 3),),
     ("near",)),
    ((),
     (),
     ("correct", 1)),
    (((1, 0, 2), (1, 1, 2), (1, 1, 3),),
     (),
     ("correct", 0)),
    (((1, 2, 2), (1, 2, 3), (1, 0, 0), (1, 0, 1), (1, 1, 0), (1, 1, 1), (1, 2, 0), (1, 2, 1), (1, 3, 1), (1, 3, 0), (1, 3, 2), (1, 3, 3),),
     ((1, 0, 2), (1, 0, 1), (1, 1, 2), (1, 0, 0), (1, 1, 3), (1, 1, 1), (1, 1, 0), (1, 2, 2), (1, 2, 0), (1, 2, 1), (1, 2, 3), (1, 3, 2), (1, 3, 3), (1, 3, 1), (1, 3, 0),),
     None),
)
F32, BF16 = jnp.float32, jnp.bfloat16


def split(value):
    high = value.astype(BF16)
    return high, (value - high.astype(F32)).astype(BF16)


def band(taps, row, size, row_sign, scale):
    rows = lax.broadcasted_iota(jnp.int32, (size, size), 0)
    cols = lax.broadcasted_iota(jnp.int32, (size, size), 1)
    count = taps.shape[2]
    offset = (cols - rows) * row_sign + (count - 1) // 2
    total = jnp.zeros((size, size), F32)
    for k in range(count):
        total = jnp.where(offset == k, taps[row, 0, k], total)
    return split(total * scale)


def kernel(dims, taps, est_in, seen_in, mask_in, out,
           est, ext, seen, mask, wsum, nums, recvs, xbuf, ymats, zmats,
           mask_sem, load_sem, halo_send, halo_recv, rs_send, rs_recv, ag_send, ag_recv):
    views, blks, bits = dims
    slab, cy, cz = seen.shape
    count = taps.shape[2]
    rad = (count - 1) // 2
    chunks = CHUNKS
    chunk = slab // chunks
    half = chunks // 2
    order = [t // 2 if t % 2 == 0 else chunks - 1 - t // 2 for t in range(chunks)]
    turn = [order.index(c) % bits for c in range(chunks)]
    v, b = lax.axis_index("view"), lax.axis_index("blk")
    bit = [(v // 2**p) % 2 for p in range(bits)]
    partner = [v + (1 - 2 * bit[p]) * 2**p for p in range(bits)]
    left, right = (b + blks - 1) % blks, (b + 1) % blks

    def planes(p):
        return pl.ds(p * chunk, chunk)

    mask_loads = [
        pltpu.make_async_copy(mask_in.at[0, planes(p)], mask.at[planes(p)], mask_sem.at[p])
        for p in range(chunks)
    ]
    loads = [
        pltpu.make_async_copy(est_in, ext.at[0, pl.ds(rad, slab)], load_sem.at[0]),
        pltpu.make_async_copy(seen_in.at[0], seen, load_sem.at[1]),
    ]
    for p in order:
        mask_loads[p].start()
    for load in loads:
        load.start()

    barrier = pltpu.get_barrier_semaphore()
    for p in range(bits):
        pl.semaphore_signal(barrier, inc=1, device_id=(partner[p], b), device_id_type=MESH)
    for near in (left, right):
        pl.semaphore_signal(barrier, inc=1, device_id=(v, near), device_id_type=MESH)

    def halo(which, side, part):
        cut = chunk if which else rad - chunk
        reach, size = ((0, cut), (cut, rad - cut))[part]
        start, land, near = (
            (slab - reach - size, rad - reach - size, right), (reach, rad + slab + reach, left))[side]
        src = ext.at[which, pl.ds(rad + start, size)] if which else est_in.at[pl.ds(start, size)]
        return pltpu.make_async_remote_copy(
            src_ref=src, dst_ref=ext.at[which, pl.ds(land, size)],
            send_sem=halo_send.at[which, side, part], recv_sem=halo_recv.at[which, side, part],
            device_id=(v, near), device_id_type=MESH)

    def halo_start(which, part):
        @pl.when(b < blks - 1)
        def _():
            halo(which, 0, part).start()

        @pl.when(b > 0)
        def _():
            halo(which, 1, part).start()

    def halo_wait(which, part):
        @pl.when(b > 0)
        def _():
            halo(which, 0, part).wait_recv()

        @pl.when(b < blks - 1)
        def _():
            halo(which, 1, part).wait_recv()

    def no_neighbour(which):
        @pl.when(b == 0)
        def _():
            ext[which, pl.ds(0, rad)] = jnp.zeros((rad, cy, cz), F32)

        @pl.when(b == blks - 1)
        def _():
            ext[which, pl.ds(rad + slab, rad)] = jnp.zeros((rad, cy, cz), F32)

    def halo_sent(which):
        for part in range(2):
            @pl.when(b < blks - 1)
            def _():
                halo(which, 0, part).wait_send()

            @pl.when(b > 0)
            def _():
                halo(which, 1, part).wait_send()

    def way(p, s):
        return (turn[p] + s) % bits

    def region(p, s):
        start, length = 0, cy
        for t in range(s):
            length //= 2
            start = start + bit[way(p, t)] * length
        return start, length

    def lines(start, length):
        if not isinstance(start, int):
            start = pl.multiple_of(start, 8)
        return pl.ds(start, length)

    def rs_copy(r, s, p):
        buf = wsum if r == 0 else nums.at[r - 1]
        start, length = region(p, s)
        length //= 2
        mine = bit[way(p, s)]
        return pltpu.make_async_remote_copy(
            src_ref=buf.at[planes(p), lines(start + (1 - mine) * length, length)],
            dst_ref=recvs.at[r, planes(p), pl.ds(cy - cy // 2**s, length)],
            send_sem=rs_send.at[r, s, p], recv_sem=rs_recv.at[r, s, p],
            device_id=(partner[way(p, s)], b), device_id_type=MESH)

    def rs_take(r, s, p):
        buf = wsum if r == 0 else nums.at[r - 1]
        rs_copy(r, s, p).wait_recv()
        start, length = region(p, s + 1)
        kept, came = lines(start, length), pl.ds(cy - cy // 2**s, length)

        def add(i, carry):
            cell = p * chunk + i
            buf[cell, kept] = buf[cell, kept] + recvs[r, cell, came]
            return carry

        lax.fori_loop(0, chunk, add, 0)

    def ag_copy(r, s, p):
        start, length = region(p, s + 1)
        if r < ITERS - 1:
            ref = est.at[r, planes(p), lines(start, length)]
        else:
            ref = out.at[planes(p), lines(start, length)]
        return pltpu.make_async_remote_copy(
            src_ref=ref, dst_ref=ref,
            send_sem=ag_send.at[r, s, p], recv_sem=ag_recv.at[r, s, p],
            device_id=(partner[way(p, s)], b), device_id_type=MESH)

    def windows(step):
        height = 8

        def run(j, carry):
            step((pl.ds(pl.multiple_of(j * height, height), height), slice(None)))
            return carry

        lax.fori_loop(0, cy // height, run, 0, unroll=2)

    def sweep(which, first, window, back, keep=None):
        totals = [None] * chunk
        for k in range(count + chunk - 1):
            if keep is not None and not keep(k):
                continue
            plane = ext[(which, first + k) + window]
            for i in range(max(0, k - count + 1), min(chunk, k + 1)):
                tap = k - i
                term = taps[0, 0, count - 1 - tap if back else tap] * plane
                totals[i] = term if totals[i] is None else totals[i] + term
        return totals

    def in_plane(cells, back):
        blurred = []
        for cell in cells:
            high, low = split(cell)
            stack = jnp.concatenate([high, high, low], axis=0)
            blurred.append(jnp.dot(ymats[back], stack, preferred_element_type=F32))
        high, low = split(jnp.concatenate(blurred, axis=0))
        high_mat, low_mat = zmats[back, 0], zmats[back, 1]
        result = jnp.dot(high, high_mat, preferred_element_type=F32)
        result += jnp.dot(low, high_mat, preferred_element_type=F32)
        result += jnp.dot(high, low_mat, preferred_element_type=F32)
        result = result.reshape(2, chunk, cy, cz)
        return result[0], result[1]

    def pair(t):
        return t, chunks - 1 - t

    def blur(which, t, back):
        for side, c in enumerate(pair(t)):
            def rows(window, side=side, c=c):
                totals = sweep(which, c * chunk, window, back)
                for i in range(chunk):
                    xbuf[(side * chunk + i,) + window] = totals[i]

            windows(rows)
        return in_plane([xbuf[i] for i in range(2 * chunk)], back)

    for p in order[:2]:
        mask_loads[p].wait()

        def to_float(i, carry):
            wsum[p * chunk + i] = mask[p * chunk + i].astype(F32)
            return carry

        lax.fori_loop(0, chunk, to_float, 0)

    pl.semaphore_wait(barrier, bits + 2)
    for p in order[:2]:
        rs_copy(0, 0, p).start()
    for part in range(2):
        halo_start(0, part)
    for p in order[2:]:
        mask_loads[p].wait()

        def to_float(i, carry):
            wsum[p * chunk + i] = mask[p * chunk + i].astype(F32)
            return carry

        lax.fori_loop(0, chunk, to_float, 0)
        rs_copy(0, 0, p).start()

    for which in range(2 * ITERS):
        no_neighbour(which)

    sums = []
    for row in range(3):
        total = taps[row, 0, 0]
        for k in range(1, count):
            total = total + taps[row, 0, k]
        sums.append(jnp.full((1, cz), total, F32))
    y_scale = (1.0 / (sums[0] * sums[1]))[:, :cy]
    z_scale = 1.0 / sums[2]
    for back in range(2):
        sign = -1 if back else 1
        high, low = band(taps, 1, cy, sign, y_scale)
        ymats[back] = jnp.concatenate([high, low, high], axis=1)
        high, low = band(taps, 2, cz, -sign, z_scale)
        zmats[back, 0] = high
        zmats[back, 1] = low
    for load in loads:
        load.wait()

    def quotient(t):
        for c, blurred in zip(pair(t), blur(0, t, 0)):
            ext[1, pl.ds(rad + c * chunk, chunk)] = seen[planes(c)] / blurred

    def spread(r):
        def step(t):
            cells = [est[r - 1, c * chunk + i] for c in pair(t) for i in range(chunk)]
            for c, blurred in zip(pair(t), in_plane(cells, 0)):
                ext[2 * r, pl.ds(rad + c * chunk, chunk)] = blurred

        return step

    low_last, high_last = (half - 1) * chunk, (half + 1) * chunk

    def divide(r, c, part):
        def late(k):
            return low_last <= c * chunk + k - rad < high_last

        keep = {"all": None, "early": lambda k: not late(k), "late": late}[part]

        def rows(window):
            totals = sweep(2 * r, c * chunk, window, 0, keep)
            for i in range(chunk):
                cell = c * chunk + i
                place = (2 * r + 1, rad + cell) + window
                total = totals[i]
                if part == "late":
                    total = ext[place] if total is None else ext[place] + total
                elif total is None:
                    total = jnp.zeros((8, cz), F32)
                ext[place] = total if part == "early" else seen[(cell,) + window] / total

        windows(rows)

    def correct(r, send):
        def step(t):
            for c, corrected in zip(pair(t), blur(2 * r + 1, t, 1)):
                nums[r, planes(c)] = mask[planes(c)].astype(F32) * corrected
            if send:
                for u in range(send):
                    @pl.when(t == u)
                    def _(u=u):
                        for p in pair(u):
                            rs_copy(r + 1, 0, p).start()

        return step

    def update(r, p):
        start, length = region(p, bits)
        kept = lines(start, length)

        def cells(i, carry):
            cell = p * chunk + i
            old = est[r - 1, cell, kept] if r else ext[0, rad + cell, kept]
            fresh = old * nums[r, cell, kept] / wsum[cell, kept]
            if r < ITERS - 1:
                est[r, cell, kept] = fresh
            else:
                out[cell, kept] = fresh
            return carry

        lax.fori_loop(0, chunk, cells, 0)

    def event(r, e, p):
        if e < bits:
            rs_take(r + 1, e, p)
            if e + 1 < bits:
                rs_copy(r + 1, e + 1, p).start()
            else:
                update(r, p)
                ag_copy(r, bits - 1, p).start()
        else:
            s = 2 * bits - 1 - e
            ag_copy(r, s, p).wait_recv()
            if s > 0:
                ag_copy(r, s - 1, p).start()

    def ordered(work, turns, before):
        def run(u, carry):
            for k in range(half):
                if k in before:
                    pl.when(u == k)(before[k])
            t = turns[0]
            for k in range(1, half):
                t = jnp.where(u == k, turns[k], t)
            work(t)
            return carry

        lax.fori_loop(0, half, run, 0)

    def near_came():
        halo_wait(0, 0)

    def far_came():
        halo_start(1, 1)
        halo_wait(0, 1)

    def weights_came():
        for p in order:
            rs_take(0, 0, p)
            if bits > 1:
                rs_copy(0, 1, p).start()
        for part in range(2):
            halo_wait(1, part)

    ordered(quotient, [*range(2, half), 1, 0], {half - 2: near_came, half - 1: far_came})
    halo_start(1, 0)
    ordered(correct(0, 2), [*range(half - 1, 1, -1), 0, 1], {half - 2: weights_came})
    for s in range(1, bits):
        for p in order:
            rs_take(0, s, p)
            if s + 1 < bits:
                rs_copy(0, s + 1, p).start()

    def step(r, stage, t):
        for p in pair(t):
            if stage < 0:
                rs_copy(r + 1, 0, p).start()
                continue
            stages = ((0,), range(1, bits), range(bits, 2 * bits - 1), (2 * bits - 1,))[stage]
            for e in stages:
                event(r, e, p)

    def compute(kind, t=0):
        if kind == "out":
            for part in range(2):
                halo_start(2, part)
        elif kind == "in":
            for part in range(2):
                halo_wait(2, part)
        elif kind == "edge":
            for c in pair(0):
                divide(1, c, "all")
            halo_start(3, 0)
        elif kind == "early":
            for u in range(1, half):
                for c in pair(u):
                    divide(1, c, "early")
        elif kind == "late":
            for u in range(t, 2 if t == 1 else half):
                for c in pair(u):
                    divide(1, c, "late")
            if t == 1:
                halo_start(3, 1)
        elif kind == "near":
            for part in range(2):
                halo_wait(3, part)

    def entry(even, odd, work):
        if even == odd:
            for item in even:
                step(*item)
        else:
            for parity, items in enumerate((even, odd)):
                @pl.when(b % 2 == parity)
                def _(items=items):
                    for item in items:
                        step(*item)
        if work and work[0] not in ("spread", "correct"):
            compute(*work)

    def entries(rows):
        def emit():
            for row in rows:
                entry(*row)

        return emit

    def looped(kind, rows, work):
        ends = [k for k, row in enumerate(rows) if row[2] and row[2][0] == kind]
        before, start = {}, 0
        for u, end in enumerate(ends):
            part = rows[start:end + 1]
            if any(row[0] or row[1] or row[2][0] != kind for row in part):
                before[u] = entries(part)
            start = end + 1
        ordered(work, [rows[k][2][1] for k in ends], before)
        return rows[start:]

    rows = looped("spread", list(SCHEDULE), spread(1))
    for k in range(len(rows)):
        if rows[k][2][0] == "correct":
            break
        entry(*rows[k])
    rows = looped("correct", rows[k:], correct(1, half))
    entries(rows)()

    for which in range(2 * ITERS):
        halo_sent(which)
    for s in range(bits):
        for p in range(chunks):
            for r in range(ITERS + 1):
                rs_copy(r, s, p).wait_send()
            for r in range(ITERS):
                ag_copy(r, s, p).wait_send()


def body(views, blks, estimate, views_seen, weight_mask, psf):
    slab, cy, cz = estimate.shape
    bits = views.bit_length() - 1
    hbm = pl.BlockSpec(memory_space=pl.ANY)
    vmem = pltpu.VMEM
    dma = pltpu.SemaphoreType.DMA
    count = psf.shape[-1]
    rad = (count - 1) // 2
    chunks = CHUNKS
    return pl.pallas_call(
        functools.partial(kernel, (views, blks, bits)),
        out_shape=vmem(estimate.shape, F32),
        in_specs=[pl.BlockSpec(memory_space=pltpu.SMEM), hbm, hbm, hbm],
        out_specs=pl.BlockSpec(memory_space=vmem),
        scratch_shapes=[
            vmem((ITERS - 1, slab, cy, cz), F32),
            vmem((2 * ITERS, slab + 2 * rad, cy, cz), F32),
            vmem((slab, cy, cz), F32),
            vmem((slab, cy, cz), jnp.int32),
            vmem((slab, cy, cz), F32),
            vmem((ITERS, slab, cy, cz), F32),
            vmem((ITERS + 1, slab, cy - cy // views, cz), F32),
            vmem((2 * (slab // chunks), cy, cz), F32),
            vmem((2, cy, 3 * cy), BF16),
            vmem((2, 2, cz, cz), BF16),
            dma((chunks,)),
            dma((2,)),
            dma((2 * ITERS, 2, 2)),
            dma((2 * ITERS, 2, 2)),
            dma((ITERS + 1, bits, chunks)),
            dma((ITERS + 1, bits, chunks)),
            dma((ITERS, bits, chunks)),
            dma((ITERS, bits, chunks)),
        ],
        compiler_params=pltpu.CompilerParams(
            collective_id=0, has_side_effects=True, vmem_limit_bytes=56 * 2**20),
    )(jnp.transpose(psf, (1, 0, 2)), estimate, views_seen, weight_mask)


def solution(mesh):
    placed = (
        P("blk", None, None),
        P("view", "blk", None, None),
        P("view", "blk", None, None),
        P("view", None, None),
    )
    return jax.shard_map(
        functools.partial(body, mesh.shape["view"], mesh.shape["blk"]),
        mesh=mesh, in_specs=placed, out_specs=P("blk", None, None), check_vma=False
    )
```
